32 devices in a mesh: rows: 8 (over z, x), rep: 4 (over y, core).
Axes of the slice: x: 2, y: 2, z: 4, core: 2. Of those that a mesh axis runs over, the one named last changes fastest.
Arguments:
- gallery: bfloat16 [8192, 1024], P('rows', 'rep'), may hold values from -6 to 6
- neighbours: int32 [8192, 10], P('rows'), may hold values from 0 to 8191, as said below
- queries: bfloat16 [128, 1024], P(None, 'rep'), may hold values from -6 to 6
- listed: int32 [128, 10], replicated, may hold values from 0 to 8191
Outputs:
- augmented: bfloat16 [8192, 1024], P('rows', 'rep')
- first_scores: float32 [128, 8192], P('rep', 'rows')
- final_scores: float32 [128, 8192], P('rep', 'rows')
The draws below stay inside these ranges and needn't reach their ends.
Inputs may be any that keep to these rules, and one draw needn't show every extreme that they name: `neighbours`: taking the rows in aligned blocks of 1024, the entries of one block name rows of another block at most 64 times and at most 32 distinct rows of it; in every draw one block is named exactly 64 times, at 32 distinct rows, by each other block.
All inputs are finite; a program needn't handle non-finite values.
Results may differ from the reference program's by a relative error of at most 0.017.
Values may be sent and summed in bfloat16 or wider, within the bound.
No kernel may reach another device: no remote copies, remote signals or barrier semaphores. Data moves between devices by JAX's collectives and lax.ppermute only.
A program may use at most 64 MiB of HBM per device.

```python
import jax
import jax.numpy as jnp
from jax import lax

D = 1024
K = 10
KQ = 10
Q = 128
ROWS_DEV = 1024
CAP = 64
UCAP = 32
N = 8192


def draw_neighbours(key, part):
    blocks = N // ROWS_DEV
    keys = jax.random.split(key, 9)
    hottest = jax.random.randint(keys[0], (), 0, blocks)
    source = jnp.arange(blocks)[:, None]
    target = jnp.arange(blocks)[None, :]
    lowest = max(1, UCAP // 4)
    distinct = jax.random.randint(keys[1], (blocks, blocks), lowest, UCAP + 1)
    distinct = jnp.where(target == hottest, UCAP, distinct)
    spread = jax.random.randint(keys[2], (blocks, blocks), 0, CAP + 1)
    counts = distinct + spread * (CAP - distinct) // CAP
    counts = jnp.where(target == hottest, CAP, counts)
    counts = jnp.where(target == source, 0, counts)
    starting = jax.random.randint(keys[3], (blocks, blocks), 0, ROWS_DEV)
    primes = jnp.array([1299709, 15485863, 32452843], jnp.int32)
    chosen = jax.random.randint(keys[4], (blocks, blocks), 0, 3)
    stride = primes[chosen] % ROWS_DEV
    places = jnp.arange(CAP)[None, None, :]
    repeats = jax.random.randint(keys[5], (blocks, blocks, CAP), 0, UCAP) % distinct[..., None]
    which_row = jnp.where(places < distinct[..., None], places, repeats)
    offsets = (starting[..., None] + which_row * stride[..., None]) % ROWS_DEV
    remote_ids = target[..., None] * ROWS_DEV + offsets
    local_ids = source[..., None] * ROWS_DEV + jax.random.randint(keys[6], (blocks, blocks, CAP), 0, ROWS_DEV)
    grid = jnp.where(places < counts[..., None], remote_ids, local_ids).reshape(blocks, blocks * CAP)
    filler = source * ROWS_DEV + jax.random.randint(keys[7], (blocks, ROWS_DEV * K - blocks * CAP), 0, ROWS_DEV)
    entries = jnp.concatenate([grid, filler], axis=1)
    shuffled = jax.vmap(lambda row_key, row_ids: jax.random.permutation(row_key, row_ids))(jax.random.split(keys[8], blocks), entries)
    return shuffled.reshape(N, K).astype(jnp.int32)


def set_ends(result, rng, least, largest):
    shape = result.shape
    index_at = [jax.random.randint(jax.random.fold_in(rng, axis), (), 0, shape[axis]) for axis in range(len(shape))]
    result = result.at[tuple(index_at)].set(least)
    longest = shape.index(max(shape))
    index_at[longest] = (index_at[longest] + 1) % shape[longest]
    return result.at[tuple(index_at)].set(largest)


def level_of(key, shape, cuts, least, largest):
    loudness, own = 1.0, jax.random.fold_in(key, 6)
    for position, shards_of in cuts:
        draws = jnp.exp(jax.random.uniform(jax.random.fold_in(own, position), (shards_of,), jnp.float32, least / len(cuts), largest / len(cuts)))
        loudness = loudness * jnp.repeat(draws, shape[position] // shards_of).reshape([-1 if axis == position else 1 for axis in range(len(shape))])
    return loudness


def gaussian(stream_key, extent, scale, reach, cuts=(), kind=jnp.bfloat16):
    values = jax.random.normal(stream_key, extent, jnp.float32) * scale
    if len(cuts) > 0:
        values = level_of(stream_key, extent, cuts, -0.22, 0.18) * values
    return jnp.clip(values, min=-reach, max=reach).astype(kind)


def setup_inputs(seed: int = 0) -> dict:
    seeds = jax.random.split(jax.random.key(seed), 5)
    gallery = gaussian(seeds[0], (N, D), 1.0, 6.0, ((0, 8), (1, 4)))
    neighbours = draw_neighbours(jax.random.fold_in(seeds[4], 71), 0)
    queries = gaussian(seeds[2], (Q, D), 1.0, 6.0, ((1, 4),))
    listed = set_ends(jax.random.randint(seeds[3], (Q, KQ), 0, N), jax.random.fold_in(seeds[3], 1), 0, N - 1).astype(jnp.int32)
    return dict(gallery=gallery, neighbours=neighbours, queries=queries, listed=listed)


epsilon = 1e-06
logit_scale = 32.0

def reference(gallery, neighbours, queries, listed):
    link_count = neighbours.shape[1]
    row_total = gallery.shape[0]
    blocks = row_total // ROWS_DEV

    def augment_block(block_index):
        start = block_index * ROWS_DEV
        summed = lax.dynamic_slice_in_dim(gallery, start, ROWS_DEV, 0).astype(jnp.float32)
        links = lax.dynamic_slice_in_dim(neighbours, start, ROWS_DEV, 0)
        for column in range(link_count):
            weight = (2 * link_count - column) / (2 * link_count)
            summed = summed + weight * gallery[links[:, column]].astype(jnp.float32)
        rounded = summed.astype(jnp.bfloat16)
        widened = rounded.astype(jnp.float32)
        return (rounded, lax.optimization_barrier(jnp.sum(widened * widened, axis=1)))
    pieces, squares = lax.map(augment_block, jnp.arange(blocks, dtype=jnp.int32))
    augmented = pieces.reshape(row_total, -1)
    row_sq = squares.reshape(row_total)
    query_wide = queries.astype(jnp.float32)
    query_sq = lax.optimization_barrier(jnp.sum(query_wide * query_wide, axis=1))
    first_dot = jnp.dot(queries, augmented.T, preferred_element_type=jnp.float32)
    first_scores = logit_scale * first_dot * lax.rsqrt(query_sq + epsilon)[:, None] * lax.rsqrt(row_sq + epsilon)[None, :]
    listed_logit = jnp.take_along_axis(first_scores, listed, axis=1)
    weights = jnp.exp(listed_logit)
    unit_rows = augmented[listed].astype(jnp.float32) * lax.rsqrt(row_sq[listed] + epsilon)[..., None]
    numer = lax.optimization_barrier(jnp.sum(weights[..., None] * unit_rows, axis=1))
    denom = lax.optimization_barrier(jnp.sum(weights, axis=1))
    expanded = query_wide * lax.rsqrt(query_sq + epsilon)[:, None] + numer / denom[:, None]
    expanded_sq = lax.optimization_barrier(jnp.sum(expanded * expanded, axis=1))
    final_dot = jnp.dot(expanded.astype(jnp.bfloat16), augmented.T, preferred_element_type=jnp.float32)
    final_scores = logit_scale * final_dot * lax.rsqrt(expanded_sq + epsilon)[:, None] * lax.rsqrt(row_sq + epsilon)[None, :]
    return (augmented, first_scores, final_scores)
```

```python
import functools

import jax
import jax.numpy as jnp
from jax import lax
from jax.experimental import pallas as pl
from jax.experimental.pallas import tpu as pltpu
from jax.sharding import PartitionSpec as P


epsilon = 1e-06
logit_scale = 32.0
LANES = 128
f32 = jnp.float32
bf16 = jnp.bfloat16
i32 = jnp.int32
VM = pl.BlockSpec(memory_space=pltpu.VMEM)
SM = pl.BlockSpec(memory_space=pltpu.SMEM)


def iota(shape, axis):
    return lax.broadcasted_iota(i32, shape, axis)


def log2(size):
    assert size & (size - 1) == 0
    return size.bit_length() - 1


def mm(a, b):
    return lax.dot_general(a, b, (((1,), (0,)), ((), ())), preferred_element_type=f32)


def mm_nt(a, b):
    return lax.dot_general(a, b, (((1,), (1,)), ((), ())), preferred_element_type=f32)


def call(body, outs, args, scratch=(), smem=(), flops=0):
    in_specs = [SM if i in smem else VM for i in range(len(args))]
    moved = sum(a.size * a.dtype.itemsize for a in args) + sum(
        o.size * o.dtype.itemsize for o in outs
    )
    return pl.pallas_call(
        body,
        out_shape=list(outs),
        in_specs=in_specs,
        out_specs=[VM] * len(outs),
        scratch_shapes=list(scratch),
        cost_estimate=pl.CostEstimate(flops=flops, bytes_accessed=moved, transcendentals=0),
        name=body.func.__name__ if isinstance(body, functools.partial) else body.__name__,
    )(*args)


def shape(dims, kind):
    return jax.ShapeDtypeStruct(dims, kind)


def presence_kernel(links_ref, out_ref):
    link_count, rows_dev = links_ref.shape
    heads = out_ref.shape[0]

    def one(k, total):
        ids = links_ref[pl.ds(k, 1), :]
        high = (ids >> 7 == iota((heads, rows_dev), 0)).astype(f32).astype(bf16)
        low = ((ids & 127) == iota((LANES, rows_dev), 0)).astype(f32).astype(bf16)
        return total + mm_nt(high, low)

    total = jnp.zeros((heads, LANES), f32)
    if heads <= 64:
        for k in range(link_count):
            total = one(k, total)
    else:
        total = lax.fori_loop(0, link_count, one, total)
    out_ref[...] = jnp.where(total > 0.5, 1.0, 0.0).astype(bf16)


def ranks(flags, chunks):
    heads = flags.shape[0]
    upper = (iota((LANES, LANES), 0) < iota((LANES, LANES), 1)).astype(f32).astype(bf16)
    ones = jnp.ones((LANES, LANES), bf16)
    row, col = iota((heads, heads), 0), iota((heads, heads), 1)
    shift = log2(chunks)
    lower = ((row >> shift == col >> shift) & (col < row)).astype(f32).astype(bf16)
    totals = mm(flags, ones).astype(bf16)
    return mm(flags, upper) + mm(lower, totals)


def pick_kernel(flags_ref, gallery_ref, out_ref, rank_ref, hot_ref):
    rows_dev = gallery_ref.shape[0]
    chunks = rows_dev // LANES
    groups = flags_ref.shape[0] // chunks
    slots = out_ref.shape[0] // groups
    flags = flags_ref[...]
    rank_ref[...] = jnp.where(flags.astype(f32) > 0.5, ranks(flags, chunks), -1.0)
    slot = iota((slots, LANES), 0).astype(f32)

    def build(group):
        for c in range(chunks):
            row = rank_ref[pl.ds(group * chunks + c, 1), :]
            hit = (row == slot).astype(f32).astype(bf16)
            start = group * slots
            if not isinstance(group, int):
                start = pl.multiple_of(start, slots)
            hot_ref[pl.ds(start, slots), c * LANES : (c + 1) * LANES] = hit

    if groups <= 8:
        for group in range(groups):
            build(group)
        out_ref[...] = mm(hot_ref[...], gallery_ref[...]).astype(bf16)
    else:
        pl.loop(0, groups)(build)
        block = 256

        @pl.loop(0, groups * slots // block)
        def _(b):
            at = pl.ds(pl.multiple_of(b * block, block), block)
            out_ref[at, :] = mm(hot_ref[at, :], gallery_ref[...]).astype(bf16)


def columns(links_ref, nb_ref):
    link_count, rows_dev = links_ref.shape
    pad = jnp.zeros((LANES - link_count, LANES), i32)
    for c in range(rows_dev // LANES):
        at = slice(c * LANES, (c + 1) * LANES)
        nb_ref[at, :] = jnp.transpose(jnp.concatenate([links_ref[:, at], pad], axis=0))


def near_kernel(me_ref, links_ref, gallery_ref, acc_ref, nb_ref, sel_ref):
    link_count, rows_dev = links_ref.shape
    first = me_ref[0] * rows_dev
    columns(links_ref, nb_ref)
    block = 32

    @pl.loop(0, rows_dev // block)
    def _(b):
        at = pl.ds(pl.multiple_of(b * block, block), block)
        ids = nb_ref[at, :] - first
        lane = iota((block, rows_dev), 1)
        own = iota((block, rows_dev), 0) + b * block
        acc = jnp.where(lane == own, 2.0 * link_count, 0.0)
        for k in range(link_count):
            acc = acc + jnp.where(ids[:, k : k + 1] == lane, 2.0 * link_count - k, 0.0)
        sel_ref[at, :] = acc.astype(bf16)

    acc_ref[...] = mm(sel_ref[...], gallery_ref[...])


def far_kernel(me_ref, links_ref, flags_ref, sel_ref, nb_ref, rank_ref):
    link_count, rows_dev = links_ref.shape
    chunks = rows_dev // LANES
    heads = flags_ref.shape[0]
    all_slots = sel_ref.shape[1]
    slots = all_slots * chunks // heads
    shift = log2(rows_dev)
    me = me_ref[0]
    columns(links_ref, nb_ref)
    flags = flags_ref[...]
    rank = ranks(flags, chunks)
    keep = (flags.astype(f32) > 0.5) & (rank < slots)
    rank_ref[...] = jnp.where(keep, rank, -1.0).astype(bf16)
    block = 128
    ones = jnp.ones((LANES, LANES), bf16)

    @pl.loop(0, rows_dev // block)
    def _(b):
        at = pl.ds(pl.multiple_of(b * block, block), block)
        ids_all = nb_ref[at, :]
        lane = iota((block, LANES), 1)
        head = iota((block, heads), 1)
        place = iota((block, all_slots), 1)
        acc = jnp.zeros((block, all_slots), f32)
        for k in range(link_count):
            ids = ids_all[:, k : k + 1]
            high = (ids >> 7 == head).astype(f32).astype(bf16)
            found = mm(high, rank_ref[...])
            found = jnp.where((ids & 127) == lane, found, 0.0).astype(bf16)
            slot = mm(found, ones)[:, :1].astype(i32)
            owner = ids >> shift
            slot = jnp.where(owner == me, -1, slot + owner * slots)
            acc = acc + jnp.where(slot == place, 2.0 * link_count - k, 0.0)
        sel_ref[at, :] = acc.astype(bf16)


def listed_kernel(me_ref, listed_ref, at_ref, which_ref, count_ref, *, width):
    list_count, queries = listed_ref.shape
    rows_dev = which_ref.shape[1]
    first = me_ref[0] * rows_dev
    group = LANES // width
    pad = jnp.full((LANES - list_count, queries), -1, i32)
    places = jnp.transpose(jnp.concatenate([listed_ref[...], pad], axis=0)) - first
    lane = iota((queries, LANES), 1)
    mine = (places >= 0) & (places < rows_dev) & (lane < list_count)
    places = jnp.where(mine, places, -1)
    for t in range(queries // 8):
        tile = places[8 * t : 8 * t + 8]
        turn = (t % group) * width
        moved = pltpu.roll(tile, turn, 1) if turn else tile
        at_ref[8 * t : 8 * t + 8, :] = jnp.where(iota((8, LANES), 1) // width == t % group, moved, -1)
        col = iota((8, rows_dev), 1)
        which = jnp.full((8, rows_dev), turn + width - 1, i32)
        count = jnp.zeros((8, rows_dev), f32)
        for k in range(list_count):
            hit = tile[:, k : k + 1] == col
            which = jnp.where(hit, turn + k, which)
            count = jnp.where(hit, count + 1.0, count)
        which_ref[8 * t : 8 * t + 8, :] = which
        count_ref[8 * t : 8 * t + 8, :] = count


def augment_kernel(
    acc_ref, sel_ref, arrived_ref, queries_ref, at_ref, aug_ref, note_ref, fp_ref, *, width, links
):
    rows_dev, features = acc_ref.shape
    queries = queries_ref.shape[0]
    chunks = rows_dev // LANES
    group = LANES // width
    total = acc_ref[...] + mm(sel_ref[...], arrived_ref[...])
    aug = (total * (0.5 / links)).astype(bf16)
    aug_ref[...] = aug
    wide = aug.astype(f32)
    square = wide * wide
    top = square.astype(bf16)
    rest = (square - top.astype(f32)).astype(bf16)
    ones = jnp.ones((16, features), bf16)
    norms = mm_nt(ones, top) + mm_nt(ones, rest)
    q = queries_ref[...]
    fp_ref[...] = mm_nt(q, aug)
    at = at_ref[...]
    low = at & 127
    high = at >> 7
    found = jnp.zeros((queries, LANES), f32)
    for c in range(chunks):
        part = jnp.take_along_axis(fp_ref[:, c * LANES : (c + 1) * LANES], low, axis=1)
        found = jnp.where(high == c, part, found)
    q_wide = q.astype(f32)
    q_sq = jnp.sum(q_wide * q_wide, axis=1, keepdims=True)
    lane = iota((8, LANES), 1)
    bands = queries // 8 // group
    for h in range(bands):
        packed = jnp.zeros((8, LANES), f32)
        for g in range(group):
            t = h * group + g
            rows = slice(8 * t, 8 * t + 8)
            packed = packed + found[rows]
            packed = jnp.where(lane == g * width + width - 2, q_sq[rows], packed)
        note_ref[8 * h : 8 * h + 8, :] = packed
    for c in range(chunks):
        note_ref[8 * bands + c : 8 * bands + c + 1, :] = norms[:1, c * LANES : (c + 1) * LANES]


def weigh_kernel(*refs, width, parts):
    notes = refs[:parts]
    which_ref, count_ref, aug_ref, out_ref, norm_ref, scale_ref, w_ref = refs[parts:]
    queries, rows_dev = which_ref.shape
    chunks = rows_dev // LANES
    group = LANES // width
    bands = queries // 8 // group
    note = notes[0][...]
    for other in notes[1:]:
        note = note + other[...]
    row_scale = lax.rsqrt(note[8 * bands : 8 * bands + chunks] + epsilon)
    norm_ref[...] = row_scale
    packed = note[: 8 * bands]
    scaled = lax.rsqrt(packed + epsilon)
    lane = iota((8, LANES), 1)
    denoms = jnp.zeros((8, LANES), f32)
    for t in range(queries // 8):
        h, g = divmod(t, group)
        rows = slice(8 * t, 8 * t + 8)
        tile = packed[8 * h : 8 * h + 8]
        at = g * width + width - 2
        query_scale = jnp.broadcast_to(scaled[8 * h : 8 * h + 8, at : at + 1], (8, LANES))
        scale_ref[rows, :] = query_scale
        denom = jnp.zeros((8, LANES), f32)
        for c in range(chunks):
            cols = slice(c * LANES, (c + 1) * LANES)
            dots = jnp.take_along_axis(tile, which_ref[rows, cols], axis=1)
            rs = row_scale[c : c + 1]
            weight = count_ref[rows, cols] * jnp.exp(logit_scale * dots * query_scale * rs)
            denom = denom + weight
            w_ref[rows, cols] = weight * rs
        denoms = jnp.where(lane == t, jnp.sum(denom, axis=1, keepdims=True), denoms)
    features = aug_ref.shape[1]
    out_ref[:queries, :] = mm(w_ref[...].astype(bf16), aug_ref[...]).astype(bf16)
    top = denoms.astype(bf16).astype(f32)
    tail = jnp.concatenate([top, denoms - top], axis=0)
    if features > LANES:
        tail = jnp.concatenate([tail, jnp.zeros((16, features - LANES), f32)], axis=1)
    out_ref[queries:, :] = tail.astype(bf16)


def total_of(refs, queries):
    rows = refs[0][:queries, :].astype(f32)
    tail = refs[0][queries:, :LANES].astype(f32)
    for ref in refs[1:]:
        rows = rows + ref[:queries, :].astype(f32)
        tail = tail + ref[queries:, :LANES].astype(f32)
    return rows, tail[:8] + tail[8:]


def join_kernel(*refs):
    out_ref = refs[-1]
    queries = out_ref.shape[0] - 16
    features = out_ref.shape[1]
    rows, denoms = total_of(refs[:-1], queries)
    out_ref[:queries, :] = rows.astype(bf16)
    top = denoms.astype(bf16).astype(f32)
    tail = jnp.concatenate([top, denoms - top], axis=0)
    if features > LANES:
        tail = jnp.concatenate([tail, jnp.zeros((16, features - LANES), f32)], axis=1)
    out_ref[queries:, :] = tail.astype(bf16)


def expand_kernel(me_ref, *refs, parts, reps, partner):
    sums = refs[:parts]
    queries_ref, scale_ref, aug_ref = refs[parts : parts + 3]
    outs = refs[parts + 3 : parts + 3 + reps]
    full_ref = refs[parts + 3 + reps]
    queries, features = queries_ref.shape
    rows_dev = aug_ref.shape[0]
    block = queries // reps
    numer, denoms = total_of(sums, queries)
    inverse = 1.0 / denoms
    pieces = []
    for t in range(queries // 8):
        rows = slice(8 * t, 8 * t + 8)
        scale = scale_ref[rows, :1]
        q = queries_ref[rows, :].astype(f32)
        pieces.append(q * scale + numer[rows] * inverse[:, t : t + 1])
    expanded = jnp.concatenate(pieces, axis=0)
    square = jnp.sum(expanded * expanded, axis=1, keepdims=True)
    top = square.astype(bf16).astype(f32)
    lane = iota((queries, LANES), 1)
    full_ref[:, :rows_dev] = mm_nt(expanded.astype(bf16), aug_ref[...]).astype(bf16)
    full_ref[:, rows_dev:] = jnp.where(lane == 0, top, square - top).astype(bf16)
    for s in range(reps):
        at = pl.multiple_of(partner(me_ref[1], s) * block, block)
        outs[s][...] = full_ref[pl.ds(at, block), :]


def final_kernel(*refs, parts):
    norm_ref, out_ref = refs[parts:]
    total = refs[0][...].astype(f32)
    for ref in refs[1:parts]:
        total = total + ref[...].astype(f32)
    block, rows_dev = out_ref.shape
    square = total[:, rows_dev : rows_dev + 1] + total[:, rows_dev + 1 : rows_dev + 2]
    scale = logit_scale * lax.rsqrt(square + epsilon)
    for c in range(rows_dev // LANES):
        cols = slice(c * LANES, (c + 1) * LANES)
        out_ref[:, cols] = total[:, cols] * scale * norm_ref[c : c + 1, :]


def split_kernel(me_ref, fp_ref, *refs, reps, partner):
    block = refs[0].shape[0]
    for s in range(reps):
        at = pl.multiple_of(partner(me_ref[1], s) * block, block)
        refs[s][...] = fp_ref[pl.ds(at, block), :].astype(bf16)


def first_kernel(me_ref, *refs, parts):
    scale_ref, norm_ref, out_ref = refs[parts:]
    block, rows_dev = out_ref.shape
    total = refs[0][...].astype(f32)
    for ref in refs[1:parts]:
        total = total + ref[...].astype(f32)
    at = pl.multiple_of(me_ref[1] * block, block)
    scale = logit_scale * scale_ref[pl.ds(at, block), :]
    for c in range(rows_dev // LANES):
        cols = slice(c * LANES, (c + 1) * LANES)
        out_ref[:, cols] = total[:, cols] * scale * norm_ref[c : c + 1, :]


def swap(value, axis, size, step):
    return lax.ppermute(value, axis, [(i, i ^ step) for i in range(size)])


def local(gallery, neighbours, queries, listed):
    rows_dev, features = gallery.shape
    query_count = queries.shape[0]
    list_count = listed.shape[1]
    links = neighbours.shape[1]
    groups = lax.axis_size("rows")
    reps = lax.axis_size("rep")
    log2(groups), log2(reps)
    chunks = rows_dev // LANES
    heads = groups * chunks
    slots = rows_dev // 32
    width = 16
    assert list_count + 2 <= width and query_count <= LANES * 8
    block = query_count // reps
    me = jnp.stack([lax.axis_index("rows"), lax.axis_index("rep")]).astype(i32)
    links_t = neighbours.T
    listed_t = listed.T

    def partner(p, s):
        return p ^ s

    (flags,) = call(presence_kernel, [shape((heads, LANES), bf16)], [links_t])
    asked = lax.all_to_all(
        flags.reshape(groups, chunks, LANES), "rows", split_axis=0, concat_axis=0, tiled=True
    ).reshape(heads, LANES)
    (acc,) = call(
        near_kernel,
        [shape((rows_dev, features), f32)],
        [me, links_t, gallery],
        [pltpu.VMEM((rows_dev, LANES), i32), pltpu.VMEM((rows_dev, rows_dev), bf16)],
        smem=(0,),
        flops=2 * rows_dev * rows_dev * features,
    )
    (picked,) = call(
        pick_kernel,
        [shape((groups * slots, features), bf16)],
        [asked, gallery],
        [pltpu.VMEM((heads, LANES), f32), pltpu.VMEM((groups * slots, rows_dev), bf16)],
        flops=2 * groups * slots * rows_dev * features,
    )
    arrived = lax.all_to_all(
        picked.reshape(groups, slots, features), "rows", split_axis=0, concat_axis=0, tiled=True
    ).reshape(groups * slots, features)
    (far,) = call(
        far_kernel,
        [shape((rows_dev, groups * slots), bf16)],
        [me, links_t, flags],
        [pltpu.VMEM((rows_dev, LANES), i32), pltpu.VMEM((heads, LANES), bf16)],
        smem=(0,),
        flops=2 * rows_dev * LANES * LANES * links,
    )
    at, which, count = call(
        functools.partial(listed_kernel, width=width),
        [
            shape((query_count, LANES), i32),
            shape((query_count, rows_dev), i32),
            shape((query_count, rows_dev), f32),
        ],
        [me, listed_t],
        smem=(0,),
    )
    bands = query_count // 8 * width // LANES
    augmented, note, first_part = call(
        functools.partial(augment_kernel, width=width, links=links),
        [
            shape((rows_dev, features), bf16),
            shape((8 * bands + chunks, LANES), f32),
            shape((query_count, rows_dev), f32),
        ],
        [acc, far, arrived, queries, at],
        flops=2 * rows_dev * features * (groups * slots + query_count),
    )
    notes = [note] + [swap(note, "rep", reps, s) for s in range(1, reps)]
    firsts = call(
        functools.partial(split_kernel, reps=reps, partner=partner),
        [shape((block, rows_dev), bf16)] * reps,
        [me, first_part],
        smem=(0,),
    )
    partial, norm, scale = call(
        functools.partial(weigh_kernel, width=width, parts=reps),
        [
            shape((query_count + 16, features), bf16),
            shape((chunks, LANES), f32),
            shape((query_count, LANES), f32),
        ],
        [*notes, which, count, augmented],
        [pltpu.VMEM((query_count, rows_dev), f32)],
        flops=2 * query_count * rows_dev * features,
    )
    sums = [partial]
    step = 1
    while step < groups:
        if len(sums) > 1:
            (total,) = call(join_kernel, [shape(partial.shape, bf16)], sums)
        else:
            total = sums[0]
        if step == 1:
            sums = [total, swap(total, "rows", groups, 1)]
            step = 2
        else:
            span = min(4, groups // step)
            sums = [total] + [swap(total, "rows", groups, step * s) for s in range(1, span)]
            step *= span
    outs = call(
        functools.partial(expand_kernel, parts=len(sums), reps=reps, partner=partner),
        [shape((block, rows_dev + LANES), bf16)] * reps,
        [me, *sums, queries, scale, augmented],
        [pltpu.VMEM((query_count, rows_dev + LANES), bf16)],
        smem=(0,),
        flops=2 * query_count * rows_dev * features,
    )
    firsts = [firsts[0]] + [swap(firsts[s], "rep", reps, s) for s in range(1, reps)]
    (first_scores,) = call(
        functools.partial(first_kernel, parts=reps),
        [shape((block, rows_dev), f32)],
        [me, *firsts, scale, norm],
        smem=(0,),
    )
    lasts = [outs[0]] + [swap(outs[s], "rep", reps, s) for s in range(1, reps)]
    (final_scores,) = call(
        functools.partial(final_kernel, parts=reps),
        [shape((block, rows_dev), f32)],
        [*lasts, norm],
    )
    return (augmented, first_scores, final_scores)


def solution(mesh):
    return jax.shard_map(
        local,
        mesh=mesh,
        in_specs=(P("rows", "rep"), P("rows", None), P(None, "rep"), P()),
        out_specs=(P("rows", "rep"), P("rep", "rows"), P("rep", "rows")),
        check_vma=False,
    )
```
